256 devices in a mesh: dp: 32 (over z, y_lo, core), tensor: 8 (over x, y_hi).
Axes of the slice: x: 4, y: 4 (y_hi: 2, y_lo: 2; y = y_hi * 2 + y_lo), z: 8, core: 2. Of those that a mesh axis runs over, the one named last changes fastest.
Arguments:
- projected: bfloat16 [3, 16384, 2560], P(None, 'dp', 'tensor'), may hold values from -40 to 40
- residue_counts: int32 [32], P('dp'), may hold values from 64 to 512, as said below
- migrate_plan: int32 [32], P('dp'), may hold values from 0 to 1, as said below
- out_weight: bfloat16 [2560, 2560], P('tensor', 'dp'), may hold values from -0.125 to 0.125
- out_cotangent: bfloat16 [64, 512, 2560], P('dp', None, 'tensor'), may hold values from -6 to 6
Outputs:
- layer_out: bfloat16 [64, 512, 2560], P('dp', None, 'tensor')
- grad_projected: bfloat16 [3, 16384, 2560], P(None, 'dp', 'tensor')
- grad_weight: float32 [2560, 2560], P('tensor', 'dp')
The draws below stay inside these ranges and needn't reach their ends.
Inputs may be any that keep to these rules, and one draw needn't show every extreme that they name: `residue_counts`: some tile has all 512 positions real, and some has exactly 64. migrate_plan[o] = 1 exactly where the sum of residue_counts over the 1 tiles of o exceeds that of its partner (o + 16) % 32 by more than 128, else 0; so never both devices of a pair have 1.
All inputs are finite; a program needn't handle non-finite values.
Results may differ from the reference program's by a relative error of at most 0.02.
Values may be sent and summed in bfloat16 or wider, within the bound.
No kernel may reach another device: no remote copies, remote signals or barrier semaphores. Data moves between devices by JAX's collectives and lax.ppermute only.
A program may use at most 128 MiB of HBM per device.

```python
import jax
import jax.numpy as jnp
from jax import lax

D = 2560
HEAD_DIM = 64
TILE = 512
HOME = 1
TILES = 32
SLOTS = 64
TOKENS = 16384
N_DP = 32
N_TENSOR = 8


def draw_projected(key, part):
    key_base = jax.random.fold_in(key, 11)
    base = jax.random.normal(key_base, (3, TOKENS, D), jnp.float32)
    scaled = jnp.concatenate([base[0:2] * 2.0, base[2:3]], axis=0)
    result = jnp.clip(scaled, -12.0, 12.0)
    return result.astype(jnp.bfloat16)


def shared_counts(key):
    drawn = jax.random.randint(jax.random.fold_in(key, 21), (TILES,), TILE // 8, TILE + 1, jnp.int32)
    drawn = drawn.at[0].set(TILE)
    drawn = drawn.at[1].set(TILE // 8)
    return drawn.astype(jnp.int32)


def draw_residue_counts(key, part):
    return shared_counts(key)


def draw_migrate_plan(key, part):
    counts = shared_counts(key)
    device_load = jnp.sum(counts.reshape(N_DP, HOME), axis=1).astype(jnp.int32)
    partner_load = jnp.roll(device_load, -(N_DP // 2))
    return (device_load > partner_load + TILE // 4).astype(jnp.int32)


def steps_of(own_key, dims, split, smallest, largest):
    loudness = 1.0
    for dim, blocks in split:
        heights = jax.random.uniform(jax.random.fold_in(jax.random.fold_in(own_key, 6), dim), (blocks,), jnp.float32, smallest / len(split), largest / len(split))
        loudness = loudness * jnp.repeat(jnp.exp(heights), dims[dim] // blocks).reshape((-1,) + (1,) * (len(dims) - 1 - dim))
    return loudness


def bell_draw(key, extent, scale, bound, pieces=(), held_as=jnp.bfloat16):
    factor_of = steps_of(key, extent, pieces, -0.22, 0.18) if pieces else 1.0
    values = jax.random.normal(key, extent, jnp.float32) * scale * factor_of
    return jnp.minimum(jnp.maximum(values, -bound), bound).astype(held_as)


def setup_inputs(seed: int = 0) -> dict:
    seeds = jax.random.split(jax.random.key(seed), 6)
    projected = draw_projected(jax.random.fold_in(seeds[5], 71), 0)
    residue_counts = draw_residue_counts(jax.random.fold_in(seeds[5], 71), 0)
    migrate_plan = draw_migrate_plan(jax.random.fold_in(seeds[5], 71), 0)
    out_weight = bell_draw(seeds[3], (D, D), D ** -0.5, 0.125, ((0, 8), (1, 32)))
    out_cotangent = bell_draw(seeds[4], (SLOTS, TILE, D), 1.0, 6.0, ((0, 32), (2, 8)))
    return dict(projected=projected, residue_counts=residue_counts, migrate_plan=migrate_plan, out_weight=out_weight, out_cotangent=out_cotangent)


def attend(tile_qkv, count):
    length = tile_qkv.shape[1]
    columns = tile_qkv.shape[2]
    head_count = columns // HEAD_DIM
    queries = tile_qkv[0].astype(jnp.float32).reshape(length, head_count, HEAD_DIM)
    key_rows = tile_qkv[1].astype(jnp.float32).reshape(length, head_count, HEAD_DIM)
    values = tile_qkv[2].astype(jnp.float32).reshape(length, head_count, HEAD_DIM)
    scores = jnp.einsum('qhd,khd->hqk', queries, key_rows) * HEAD_DIM ** (-0.5)
    position = lax.iota(jnp.int32, length)
    live_mask = position < count
    scores = jnp.where(live_mask[None, None, :], scores, -1000000000.0)
    row_max = lax.optimization_barrier(jnp.max(scores, axis=2, keepdims=True))
    exponent = jnp.exp(scores - row_max)
    weights = (exponent / lax.optimization_barrier(jnp.sum(exponent, axis=2, keepdims=True))).astype(jnp.bfloat16)
    context = jnp.einsum('hqk,khd->qhd', weights.astype(jnp.float32), values)
    context = context * live_mask.astype(jnp.float32)[:, None, None]
    return context.reshape(length, columns)

def reference(projected, residue_counts, migrate_plan, out_weight, out_cotangent):
    tiles_all = N_DP * HOME
    slots_all = N_DP * (HOME + 1)
    group_width = D // N_TENSOR
    home_qkv = jnp.transpose(projected.reshape(3, tiles_all, TILE, D), (1, 0, 2, 3))
    context = lax.map(lambda packed: attend(packed[0], packed[1]).astype(jnp.bfloat16), (home_qkv, residue_counts))
    owner_dev = lax.iota(jnp.int32, tiles_all) // HOME
    home_place = lax.iota(jnp.int32, tiles_all) % HOME
    migrated = (home_place == HOME - 1) & (migrate_plan[owner_dev] == 1)
    helper = (owner_dev + N_DP // 2) % N_DP
    slot_index = jnp.where(migrated, helper * (HOME + 1) + HOME, owner_dev * (HOME + 1) + home_place).astype(jnp.int32)
    placed = jnp.zeros((slots_all, TILE, D), jnp.bfloat16).at[slot_index].set(context)
    flat_ctx = placed.reshape(slots_all * TILE, D)
    running = jnp.zeros((slots_all * TILE, D), jnp.float32)
    for block_index in range(N_TENSOR):
        lower = block_index * group_width
        partial_value = jnp.dot(flat_ctx[:, lower:lower + group_width], out_weight[lower:lower + group_width], preferred_element_type=jnp.float32)
        partial_value = lax.optimization_barrier(partial_value.astype(jnp.bfloat16)).astype(jnp.float32)
        running = running + partial_value
    layer_out = running.astype(jnp.bfloat16).reshape(slots_all, TILE, D)
    flat_cot = out_cotangent.reshape(slots_all * TILE, D)
    grad_context = jnp.dot(flat_cot, out_weight.T, preferred_element_type=jnp.float32).astype(jnp.bfloat16)
    grad_context = grad_context.reshape(slots_all, TILE, D)
    grad_weight = jnp.dot(flat_ctx.T, flat_cot, preferred_element_type=jnp.float32)
    cotangent = grad_context[slot_index]

    def tile_back(packed):
        tile_qkv, count, tile_cot = packed
        _, pullback = jax.vjp(lambda operand: attend(operand, count), tile_qkv)
        return pullback(tile_cot.astype(jnp.float32))[0]
    slot_grads = lax.map(tile_back, (home_qkv, residue_counts, cotangent))
    grad_projected = jnp.transpose(slot_grads, (1, 0, 2, 3)).reshape(3, tiles_all * TILE, D).astype(jnp.bfloat16)
    return (layer_out, grad_projected, grad_weight)
```

```python
import functools

import jax
import jax.numpy as jnp
from jax import lax
from jax.experimental import pallas as pl
from jax.experimental.pallas import tpu as pltpu
from jax.sharding import PartitionSpec as P

HEAD_DIM = 64
N_DP = 32
N_TENSOR = 8
X = N_TENSOR // 2
Z = N_DP // 4
BF16 = jnp.bfloat16
F32 = jnp.float32


SMEM = pl.BlockSpec(memory_space=pltpu.SMEM)
VMEM = pl.BlockSpec(memory_space=pltpu.VMEM)

PLACES = ((0, 0), (1, 0), (-1, 0), (2, 0), (0, 1), (1, 1), (-1, 1), (2, 1))


def dot(a, b, dim_a, dim_b):
    return lax.dot_general(a, b, (((dim_a,), (dim_b,)), ((), ())), preferred_element_type=F32)


def along_dp(value, to):
    return lax.ppermute(value, "dp", [(i, to(i)) for i in range(N_DP)])


def along_tensor(value, dx, dy):
    def to(i):
        return ((i // 2 + dx) % X) * 2 + ((i % 2) ^ dy)

    return lax.ppermute(value, "tensor", [(i, to(i)) for i in range(N_TENSOR)])


def swapped(value):
    pairs = []
    for a in range(Z):
        for j in range(4):
            for b in range(N_TENSOR):
                pairs.append(((4 * a + j) * N_TENSOR + b, (4 * b + j) * N_TENSOR + a))
    return lax.ppermute(value, ("dp", "tensor"), pairs)


def tensor_place(dx, dy):
    t = lax.axis_index("tensor")
    return lax.rem(t // 2 + (dx + X), X) * 2 + lax.rem(lax.rem(t, 2) + dy, 2)


def probs_of(q, k, count):
    scores = dot(k, q, 0, 0)
    rows = lax.broadcasted_iota(jnp.int32, scores.shape, 0)
    scores = jnp.where(rows < count, scores, -1000000000.0)
    exponent = jnp.exp(scores - jnp.max(scores, axis=0, keepdims=True))
    return exponent * (1.0 / jnp.sum(exponent, axis=0, keepdims=True))


def forward_kernel(count_ref, qkv_ref, ctx_ref):
    count = count_ref[0]
    live = lax.broadcasted_iota(jnp.int32, (1, ctx_ref.shape[1]), 1) < count
    q = qkv_ref[0] * jnp.asarray(HEAD_DIM ** (-0.5), BF16)
    probs = probs_of(q, qkv_ref[1], count).astype(BF16)
    context = dot(qkv_ref[2], probs, 1, 0)
    ctx_ref[...] = jnp.where(live, context, 0.0).astype(BF16)


def backward_kernel(count_ref, qkv_ref, *refs):
    grad_refs, out_ref = refs[:-1], refs[-1]
    count = count_ref[0]
    grad = functools.reduce(lambda a, b: a + b, [r[...].astype(F32) for r in grad_refs])
    live = lax.broadcasted_iota(jnp.int32, (1, grad.shape[1]), 1) < count
    grad = jnp.where(live, grad, 0.0).astype(BF16)
    scale = jnp.asarray(HEAD_DIM ** (-0.5), BF16)
    q, k, v = qkv_ref[0] * scale, qkv_ref[1], qkv_ref[2]
    probs = probs_of(q, k, count)
    out_ref[2] = dot(grad, probs.astype(BF16), 1, 1).astype(BF16)
    grad_probs = dot(v, grad, 0, 0).astype(BF16).astype(F32)
    inner = jnp.sum(probs * grad_probs, axis=0, keepdims=True)
    grad_scores = (probs * (grad_probs - inner)).astype(BF16)
    out_ref[0] = (dot(k, grad_scores, 1, 0) * HEAD_DIM ** (-0.5)).astype(BF16)
    out_ref[1] = dot(q, grad_scores, 1, 1).astype(BF16)


def heads_call(kernel, name, count, qkv, grads, out_planes):
    _, columns, length = qkv.shape
    heads = columns // HEAD_DIM
    plane = pl.BlockSpec((HEAD_DIM, length), lambda h: (h, 0))
    planes = pl.BlockSpec((3, HEAD_DIM, length), lambda h: (0, h, 0))
    dots = 6 if out_planes else 2
    return pl.pallas_call(
        kernel,
        name=name,
        grid=(heads,),
        in_specs=[SMEM, planes] + [plane] * len(grads),
        out_specs=planes if out_planes else plane,
        out_shape=jax.ShapeDtypeStruct(
            (3, columns, length) if out_planes else (columns, length), BF16
        ),
        cost_estimate=pl.CostEstimate(
            flops=2 * dots * columns * length * length,
            bytes_accessed=8 * columns * length * 2,
            transcendentals=heads * length * length,
        ),
    )(count, qkv, *grads)


def grad_partial_kernel(cot_ref, w0_ref, wy_ref, wc_ref, wcy_ref, all_ref, *out_refs):
    dp = lax.axis_index("dp")
    z, j = dp // 4, lax.rem(dp, 4)
    yl, c = j // 2, lax.rem(j, 2)
    for ref, flip_y, flip_c in ((w0_ref, 0, 0), (wy_ref, 1, 0), (wc_ref, 0, 1), (wcy_ref, 1, 1)):
        col = lax.rem(yl + flip_y, 2) * 2 + lax.rem(c + flip_c, 2)
        for k in range(Z):
            all_ref[lax.rem(z + Z - k, Z), col] = ref[k]
    for (dx, dy), out_ref in zip(PLACES, out_refs):
        block = all_ref[tensor_place(dx, dy)].reshape(-1, all_ref.shape[3])
        out_ref[...] = dot(block, cot_ref[...], 0, 0).astype(BF16)


def grad_partial(cot, w0, wy, wc, wcy):
    columns, length = cot.shape
    rows = w0.shape[2]
    return pl.pallas_call(
        grad_partial_kernel,
        name="grad_partial",
        in_specs=[VMEM] * 5,
        out_specs=[VMEM] * 9,
        out_shape=[jax.ShapeDtypeStruct((Z, 4, columns // 4, rows), BF16)]
        + [jax.ShapeDtypeStruct((rows, length), BF16)] * 8,
        cost_estimate=pl.CostEstimate(
            flops=2 * 8 * columns * rows * length, bytes_accessed=8_000_000, transcendentals=0
        ),
    )(cot, w0, wy, wc, wcy)


def layer_out_kernel(flag_ref, all_ref, *refs):
    block_refs, (home_ref, guest_ref) = refs[:-2], refs[-2:]
    total = None
    for (dx, dy), block_ref in zip(PLACES, block_refs):
        weight = all_ref[tensor_place(dx, dy)].reshape(-1, all_ref.shape[3])
        term = dot(weight, block_ref[...], 1, 0)
        total = term if total is None else total + term
    sent = flag_ref[0] > 0
    home_ref[...] = jnp.where(sent, 0.0, total).astype(BF16)
    guest_ref[...] = jnp.where(sent, total, 0.0).astype(BF16)


def layer_out_of(flag, weight, blocks):
    rows, length = blocks[0].shape
    columns = 4 * weight.shape[2]
    return pl.pallas_call(
        layer_out_kernel,
        name="layer_out",
        in_specs=[SMEM, VMEM] + [VMEM] * 8,
        out_specs=[VMEM] * 2,
        out_shape=[jax.ShapeDtypeStruct((columns, length), BF16)] * 2,
        cost_estimate=pl.CostEstimate(
            flops=2 * 8 * columns * rows * length, bytes_accessed=6_000_000, transcendentals=0
        ),
    )(flag, weight, *blocks)


def weight_partial_kernel(cot_ref, *refs):
    block_refs, (keep_ref, send_ref, held) = refs[:-3], refs[-3:]
    dp = lax.axis_index("dp")
    z, j = dp // 4, lax.rem(dp, 4)
    yl, c = j // 2, lax.rem(j, 2)
    for (dx, dy), block_ref in zip(PLACES, block_refs):
        held[...] = dot(cot_ref[...], block_ref[...], 1, 1).astype(BF16).reshape(held.shape)
        k = lax.rem(tensor_place(dx, dy) + Z - z, Z)
        for out_ref, flip_c in ((keep_ref, 0), (send_ref, 1)):
            for flip_y in range(2):
                col = lax.rem(yl + flip_y, 2) * 2 + lax.rem(c + flip_c, 2)
                out_ref[flip_y, k] = held[col]


def weight_partial(cot, blocks):
    columns, length = cot.shape
    rows = blocks[0].shape[0]
    out = jax.ShapeDtypeStruct((2, Z, columns // 4, rows), BF16)
    return pl.pallas_call(
        weight_partial_kernel,
        name="weight_partial",
        in_specs=[VMEM] * 9,
        out_specs=[VMEM] * 2,
        out_shape=[out, out],
        scratch_shapes=[pltpu.VMEM((4, columns // 4, rows), BF16)],
        cost_estimate=pl.CostEstimate(
            flops=2 * 8 * columns * rows * length, bytes_accessed=6_000_000, transcendentals=0
        ),
    )(cot, *blocks)


def added(*terms):
    return functools.reduce(lambda a, b: a + b, [t.astype(F32) for t in terms]).astype(BF16)


def shards(projected, residue_counts, migrate_plan, out_weight, out_cotangent):
    qkv = jnp.transpose(projected, (0, 2, 1))
    cot_slots = jnp.transpose(out_cotangent, (0, 2, 1))
    weight_shard = out_weight.T
    sent = migrate_plan[0] > 0

    moved = swapped(weight_shard)
    guest_cot = along_dp(cot_slots[1], lambda i: (i + N_DP // 2) % N_DP)

    ctx = heads_call(forward_kernel, "forward", residue_counts, qkv, (), False)

    block = {(0, 0): ctx}
    block[0, 1] = along_tensor(ctx, 0, 1)
    block[-1, 0] = along_tensor(ctx, 1, 0)
    block[1, 0] = along_tensor(ctx, -1, 0)
    block[2, 0] = along_tensor(ctx, 2, 0)
    block[-1, 1] = along_tensor(block[0, 1], 1, 0)
    block[1, 1] = along_tensor(block[0, 1], -1, 0)
    block[2, 1] = along_tensor(block[2, 0], 0, 1)
    blocks = [block[place] for place in PLACES]

    line = [moved]
    for k in range(1, Z):
        line.append(along_dp(moved, lambda i, k=k: (i + 4 * k) % N_DP))
    w0 = jnp.stack(line)
    wc = along_dp(w0, lambda i: i ^ 1)
    wy = along_dp(w0, lambda i: i ^ 2)
    wcy = along_dp(wy, lambda i: i ^ 1)

    cot = jnp.where(sent, guest_cot, cot_slots[0])
    weight, *parts = grad_partial(cot, w0, wy, wc, wcy)
    part = dict(zip(PLACES, parts))

    from_left = along_tensor(part[1, 1], 1, 0)
    from_right = along_tensor(part[-1, 1], -1, 0)
    from_other = along_tensor(part[2, 1], 0, 1)
    got = [along_tensor(part[1, 0], 1, 0), along_tensor(part[-1, 0], -1, 0)]
    got.append(along_tensor(added(part[2, 0], from_other), 2, 0))
    got.append(along_tensor(added(part[0, 1], from_left, from_right), 0, 1))

    keep, send = weight_partial(cot, blocks)
    both = along_dp(send, lambda i: i ^ 1)
    other_y = along_dp(added(keep[1], both[1]), lambda i: i ^ 2)
    summed = added(keep[0], both[0], other_y)
    terms = [summed[0]]
    for k in range(1, Z):
        terms.append(along_dp(summed[k], lambda i, k=k: (i + 4 * k) % N_DP))
    grad_weight = swapped(added(*terms)).astype(F32).T

    home, guest = layer_out_of(migrate_plan, weight, blocks)
    returned = along_dp(guest, lambda i: (i + N_DP // 2) % N_DP)
    layer_out = jnp.transpose(jnp.stack([home, returned]), (0, 2, 1))

    grad_qkv = heads_call(
        backward_kernel, "backward", residue_counts, qkv, (part[0, 0], *got), True
    )
    return layer_out, jnp.transpose(grad_qkv, (0, 2, 1)), grad_weight


def solution(mesh):
    in_specs = (
        P(None, "dp", "tensor"),
        P("dp"),
        P("dp"),
        P("tensor", "dp"),
        P("dp", None, "tensor"),
    )
    out_specs = (P("dp", None, "tensor"), P(None, "dp", "tensor"), P("tensor", "dp"))
    return jax.shard_map(shards, mesh=mesh, in_specs=in_specs, out_specs=out_specs, check_vma=False)
```

```python
import functools

import jax
import jax.numpy as jnp
from jax import lax
from jax.experimental import pallas as pl
from jax.experimental.pallas import tpu as pltpu
from jax.sharding import PartitionSpec as P


HEAD_DIM = 64
N_DP = 32
N_TENSOR = 8
X = N_TENSOR // 2
Z = N_DP // 4
BF16 = jnp.bfloat16
F32 = jnp.float32


SMEM = pl.BlockSpec(memory_space=pltpu.SMEM)
VMEM = pl.BlockSpec(memory_space=pltpu.VMEM)

PLACES = ((0, 0), (1, 0), (-1, 0), (2, 0), (0, 1), (1, 1), (-1, 1), (2, 1))

APART = (0, 4, 2, 6, 1, 5, 3, 7)


def dot(a, b, dim_a, dim_b):
    return lax.dot_general(a, b, (((dim_a,), (dim_b,)), ((), ())), preferred_element_type=F32)


def along_dp(value, to):
    return lax.ppermute(value, "dp", [(i, to(i)) for i in range(N_DP)])


def along_tensor(value, dx, dy):
    def to(i):
        return ((i // 2 + dx) % X) * 2 + ((i % 2) ^ dy)

    return lax.ppermute(value, "tensor", [(i, to(i)) for i in range(N_TENSOR)])


def swapped(value):
    pairs = []
    for a in range(Z):
        for j in range(4):
            for b in range(N_TENSOR):
                pairs.append(((4 * a + j) * N_TENSOR + b, (4 * b + j) * N_TENSOR + a))
    return lax.ppermute(value, ("dp", "tensor"), pairs)


def exchanged(value, flip):
    return along_dp(value, lambda i: i ^ flip)


def half_round(value):
    return along_dp(value, lambda i: (i + N_DP // 2) % N_DP)


def tensor_place(dx, dy):
    t = lax.axis_index("tensor")
    return lax.rem(t // 2 + (dx + X), X) * 2 + lax.rem(lax.rem(t, 2) + dy, 2)


def probs_of(q, k, count):
    scores = dot(k, q, 0, 0)
    rows = lax.broadcasted_iota(jnp.int32, scores.shape, 0)
    scores = jnp.where(rows < count, scores, -1000000000.0)
    exponent = jnp.exp(scores - jnp.max(scores, axis=0, keepdims=True))
    return exponent * (1.0 / jnp.sum(exponent, axis=0, keepdims=True))


def forward_kernel(count_ref, qkv_ref, ctx_ref):
    count = count_ref[0]
    live = lax.broadcasted_iota(jnp.int32, (1, ctx_ref.shape[1]), 1) < count
    q = qkv_ref[0] * jnp.asarray(HEAD_DIM ** (-0.5), BF16)
    probs = probs_of(q, qkv_ref[1], count).astype(BF16)
    context = dot(qkv_ref[2], probs, 1, 0)
    ctx_ref[...] = jnp.where(live, context, 0.0).astype(BF16)


def backward_kernel(count_ref, qkv_ref, *refs):
    grad_refs, out_ref = refs[:-1], refs[-1]
    count = count_ref[0]
    grad = functools.reduce(lambda a, b: a + b, [r[...].astype(F32) for r in grad_refs])
    live = lax.broadcasted_iota(jnp.int32, (1, grad.shape[1]), 1) < count
    grad = jnp.where(live, grad, 0.0).astype(BF16)
    scale = jnp.asarray(HEAD_DIM ** (-0.5), BF16)
    q, k, v = qkv_ref[0] * scale, qkv_ref[1], qkv_ref[2]
    probs = probs_of(q, k, count)
    out_ref[2] = dot(grad, probs.astype(BF16), 1, 1).astype(BF16)
    grad_probs = dot(v, grad, 0, 0).astype(BF16).astype(F32)
    inner = jnp.sum(probs * grad_probs, axis=0, keepdims=True)
    grad_scores = (probs * (grad_probs - inner)).astype(BF16)
    out_ref[0] = (dot(k, grad_scores, 1, 0) * HEAD_DIM ** (-0.5)).astype(BF16)
    out_ref[1] = dot(q, grad_scores, 1, 1).astype(BF16)


def heads_call(kernel, count, qkv, grads, out_planes):
    _, columns, length = qkv.shape
    heads = columns // HEAD_DIM
    plane = pl.BlockSpec((HEAD_DIM, length), lambda h: (h, 0))
    planes = pl.BlockSpec((3, HEAD_DIM, length), lambda h: (0, h, 0))
    dots = 6 if out_planes else 2
    return pl.pallas_call(
        kernel,
        grid=(heads,),
        in_specs=[SMEM, planes] + [plane] * len(grads),
        out_specs=planes if out_planes else plane,
        out_shape=jax.ShapeDtypeStruct(
            (3, columns, length) if out_planes else (columns, length), BF16
        ),
        cost_estimate=pl.CostEstimate(
            flops=2 * dots * columns * length * length,
            bytes_accessed=8 * columns * length * 2,
            transcendentals=heads * length * length,
        ),
    )(count, qkv, *grads)


def grad_partial_kernel(cot_ref, w0_ref, wy_ref, wc_ref, wcy_ref, all_ref, *out_refs):
    dp = lax.axis_index("dp")
    z, j = dp // 4, lax.rem(dp, 4)
    yl, c = j // 2, lax.rem(j, 2)
    for ref, flip_y, flip_c in ((w0_ref, 0, 0), (wy_ref, 1, 0), (wc_ref, 0, 1), (wcy_ref, 1, 1)):
        col = lax.rem(yl + flip_y, 2) * 2 + lax.rem(c + flip_c, 2)
        for k, apart in enumerate(APART):
            all_ref[z ^ apart, col] = ref[k]
    for (dx, dy), out_ref in zip(PLACES, out_refs):
        block = all_ref[tensor_place(dx, dy)].reshape(-1, all_ref.shape[3])
        out_ref[...] = dot(block, cot_ref[...], 0, 0).astype(BF16)


def grad_partial(cot, w0, wy, wc, wcy):
    columns, length = cot.shape
    rows = w0.shape[2]
    return pl.pallas_call(
        grad_partial_kernel,
        name="grad_partial",
        in_specs=[VMEM] * 5,
        out_specs=[VMEM] * 9,
        out_shape=[jax.ShapeDtypeStruct((Z, 4, columns // 4, rows), BF16)]
        + [jax.ShapeDtypeStruct((rows, length), BF16)] * 8,
        cost_estimate=pl.CostEstimate(
            flops=2 * 8 * columns * rows * length, bytes_accessed=8_000_000, transcendentals=0
        ),
    )(cot, w0, wy, wc, wcy)


def layer_out_kernel(flag_ref, all_ref, *refs):
    block_refs, (home_ref, guest_ref) = refs[:-2], refs[-2:]
    total = None
    for (dx, dy), block_ref in zip(PLACES, block_refs):
        weight = all_ref[tensor_place(dx, dy)].reshape(-1, all_ref.shape[3])
        term = dot(weight, block_ref[...], 1, 0)
        total = term if total is None else total + term
    sent = flag_ref[0] > 0
    home_ref[...] = jnp.where(sent, 0.0, total).astype(BF16)
    guest_ref[...] = jnp.where(sent, total, 0.0).astype(BF16)


def layer_out_of(flag, weight, blocks):
    rows, length = blocks[0].shape
    columns = 4 * weight.shape[2]
    return pl.pallas_call(
        layer_out_kernel,
        name="layer_out",
        in_specs=[SMEM, VMEM] + [VMEM] * 8,
        out_specs=[VMEM] * 2,
        out_shape=[jax.ShapeDtypeStruct((columns, length), BF16)] * 2,
        cost_estimate=pl.CostEstimate(
            flops=2 * 8 * columns * rows * length, bytes_accessed=6_000_000, transcendentals=0
        ),
    )(flag, weight, *blocks)


def weight_partial_kernel(cot_ref, *refs):
    block_refs, (keep_ref, send_ref, held) = refs[:-3], refs[-3:]
    dp = lax.axis_index("dp")
    z, j = dp // 4, lax.rem(dp, 4)
    yl, c = j // 2, lax.rem(j, 2)
    for (dx, dy), block_ref in zip(PLACES, block_refs):
        held[...] = dot(cot_ref[...], block_ref[...], 1, 1).astype(BF16).reshape(held.shape)
        apart = tensor_place(dx, dy) ^ z
        k = lax.rem(apart, 2) * 4 + lax.rem(apart // 2, 2) * 2 + apart // 4
        for out_ref, flip_c in ((keep_ref, 0), (send_ref, 1)):
            for flip_y in range(2):
                col = lax.rem(yl + flip_y, 2) * 2 + lax.rem(c + flip_c, 2)
                out_ref[flip_y, k] = held[col]


def weight_partial(cot, blocks):
    columns, length = cot.shape
    rows = blocks[0].shape[0]
    out = jax.ShapeDtypeStruct((2, Z, columns // 4, rows), BF16)
    return pl.pallas_call(
        weight_partial_kernel,
        name="weight_partial",
        in_specs=[VMEM] * 9,
        out_specs=[VMEM] * 2,
        out_shape=[out, out],
        scratch_shapes=[pltpu.VMEM((4, columns // 4, rows), BF16)],
        cost_estimate=pl.CostEstimate(
            flops=2 * 8 * columns * rows * length, bytes_accessed=6_000_000, transcendentals=0
        ),
    )(cot, *blocks)


def added(*terms):
    return functools.reduce(lambda a, b: a + b, [t.astype(F32) for t in terms]).astype(BF16)


def step(projected, residue_counts, migrate_plan, out_weight, out_cotangent):
    qkv = jnp.transpose(projected, (0, 2, 1))
    cot_slots = jnp.transpose(out_cotangent, (0, 2, 1))
    sent = migrate_plan[0] > 0

    moved = swapped(out_weight.T)
    guest_cot = half_round(cot_slots[1])

    ctx = heads_call(forward_kernel, residue_counts, qkv, (), False)

    block = {(0, 0): ctx}
    block[0, 1] = along_tensor(ctx, 0, 1)
    block[2, 0] = along_tensor(ctx, 2, 0)
    block[-1, 0] = along_tensor(ctx, 1, 0)
    block[1, 0] = along_tensor(ctx, -1, 0)
    block[-1, 1] = along_tensor(block[0, 1], 1, 0)
    block[1, 1] = along_tensor(block[0, 1], -1, 0)
    block[2, 1] = along_tensor(block[2, 0], 0, 1)
    blocks = [block[place] for place in PLACES]

    stack = moved[None]
    for bit in (4, 2, 1):
        stack = jnp.concatenate([stack, exchanged(stack, 4 * bit)])
    w0 = stack
    wy = exchanged(w0, 2)
    wc = exchanged(w0, 1)
    wcy = exchanged(wy, 1)

    cot = jnp.where(sent, guest_cot, cot_slots[0])
    weight, *parts = grad_partial(cot, w0, wy, wc, wcy)
    part = dict(zip(PLACES, parts))

    from_other = along_tensor(part[2, 1], 0, 1)
    from_left = along_tensor(part[1, 1], 1, 0)
    from_right = along_tensor(part[-1, 1], -1, 0)
    got = [along_tensor(part[1, 0], 1, 0), along_tensor(part[-1, 0], -1, 0)]
    got.append(along_tensor(added(part[2, 0], from_other), 2, 0))
    got.append(along_tensor(added(part[0, 1], from_left, from_right), 0, 1))

    keep, send = weight_partial(cot, blocks)
    both = exchanged(send, 1)
    total = added(keep[0], both[0], exchanged(added(keep[1], both[1]), 2))
    for bit in (1, 2, 4):
        half = total.shape[0] // 2
        total = added(total[:half], exchanged(total[half:], 4 * bit))
    grad_weight = swapped(total[0]).astype(F32).T

    home, guest = layer_out_of(migrate_plan, weight, blocks)
    returned = half_round(guest)
    layer_out = jnp.transpose(jnp.stack([home, returned]), (0, 2, 1))

    grad_qkv = heads_call(backward_kernel, residue_counts, qkv, (part[0, 0], *got), True)
    return layer_out, jnp.transpose(grad_qkv, (0, 2, 1)), grad_weight


def solution(mesh):
    in_specs = (
        P(None, "dp", "tensor"),
        P("dp"),
        P("dp"),
        P("tensor", "dp"),
        P("dp", None, "tensor"),
    )
    out_specs = (P("dp", None, "tensor"), P(None, "dp", "tensor"), P("tensor", "dp"))
    return jax.shard_map(step, mesh=mesh, in_specs=in_specs, out_specs=out_specs, check_vma=False)
```

```python
import functools

import jax
import jax.numpy as jnp
from jax import lax
from jax.experimental import pallas as pl
from jax.experimental.pallas import tpu as pltpu
from jax.sharding import PartitionSpec as P


HEAD_DIM = 64
N_DP = 32
N_TENSOR = 8
X = N_TENSOR // 2
Z = N_DP // 4
BF16 = jnp.bfloat16
F32 = jnp.float32


SMEM = pl.BlockSpec(memory_space=pltpu.SMEM)
VMEM = pl.BlockSpec(memory_space=pltpu.VMEM)

PLACES = ((0, 0), (1, 0), (-1, 0), (2, 0), (0, 1), (1, 1), (-1, 1), (2, 1))

APART = (0, 4, 2, 6, 1, 5, 3, 7)


def dot(a, b, dim_a, dim_b):
    return lax.dot_general(a, b, (((dim_a,), (dim_b,)), ((), ())), preferred_element_type=F32)


def along_dp(value, to):
    return lax.ppermute(value, "dp", [(i, to(i)) for i in range(N_DP)])


def along_tensor(value, dx, dy):
    def to(i):
        return ((i // 2 + dx) % X) * 2 + ((i % 2) ^ dy)

    return lax.ppermute(value, "tensor", [(i, to(i)) for i in range(N_TENSOR)])


def swapped(value, flip):
    pairs = []
    for a in range(Z):
        for j in range(4):
            for b in range(N_TENSOR):
                pairs.append(((4 * a + j) * N_TENSOR + b, (4 * (b ^ flip) + j) * N_TENSOR + a))
    return lax.ppermute(value, ("dp", "tensor"), pairs)


def swapped_back(value, flip):
    pairs = []
    for a in range(Z):
        for j in range(4):
            for b in range(N_TENSOR):
                pairs.append(((4 * a + j) * N_TENSOR + b, (4 * b + j) * N_TENSOR + (a ^ flip)))
    return lax.ppermute(value, ("dp", "tensor"), pairs)


def exchanged(value, flip):
    return along_dp(value, lambda i: i ^ flip)


def half_round(value):
    return along_dp(value, lambda i: (i + N_DP // 2) % N_DP)


def tensor_place(dx, dy):
    t = lax.axis_index("tensor")
    return lax.rem(t // 2 + (dx + X), X) * 2 + lax.rem(lax.rem(t, 2) + dy, 2)


def probs_of(q, k, count):
    scores = dot(k, q, 0, 0)
    rows = lax.broadcasted_iota(jnp.int32, scores.shape, 0)
    scores = jnp.where(rows < count, scores, -1000000000.0)
    exponent = jnp.exp(scores - jnp.max(scores, axis=0, keepdims=True))
    return exponent * (1.0 / jnp.sum(exponent, axis=0, keepdims=True))


def forward_kernel(count_ref, qkv_ref, ctx_ref):
    count = count_ref[0]
    live = lax.broadcasted_iota(jnp.int32, (1, ctx_ref.shape[1]), 1) < count
    q = qkv_ref[0] * jnp.asarray(HEAD_DIM ** (-0.5), BF16)
    probs = probs_of(q, qkv_ref[1], count).astype(BF16)
    context = dot(qkv_ref[2], probs, 1, 0)
    ctx_ref[...] = jnp.where(live, context, 0.0).astype(BF16)


def backward_kernel(count_ref, qkv_ref, *refs):
    grad_refs, out_ref = refs[:-1], refs[-1]
    count = count_ref[0]
    grad = functools.reduce(lambda a, b: a + b, [r[...].astype(F32) for r in grad_refs])
    live = lax.broadcasted_iota(jnp.int32, (1, grad.shape[1]), 1) < count
    grad = jnp.where(live, grad, 0.0).astype(BF16)
    scale = jnp.asarray(HEAD_DIM ** (-0.5), BF16)
    q, k, v = qkv_ref[0] * scale, qkv_ref[1], qkv_ref[2]
    probs = probs_of(q, k, count)
    out_ref[2] = dot(grad, probs.astype(BF16), 1, 1).astype(BF16)
    grad_probs = dot(v, grad, 0, 0).astype(BF16).astype(F32)
    inner = jnp.sum(probs * grad_probs, axis=0, keepdims=True)
    grad_scores = (probs * (grad_probs - inner)).astype(BF16)
    out_ref[0] = (dot(k, grad_scores, 1, 0) * HEAD_DIM ** (-0.5)).astype(BF16)
    out_ref[1] = dot(q, grad_scores, 1, 1).astype(BF16)


def heads_call(kernel, count, qkv, grads, out_planes):
    _, columns, length = qkv.shape
    heads = columns // HEAD_DIM
    plane = pl.BlockSpec((HEAD_DIM, length), lambda h: (h, 0))
    planes = pl.BlockSpec((3, HEAD_DIM, length), lambda h: (0, h, 0))
    dots = 6 if out_planes else 2
    return pl.pallas_call(
        kernel,
        grid=(heads,),
        in_specs=[SMEM, planes] + [plane] * len(grads),
        out_specs=planes if out_planes else plane,
        out_shape=jax.ShapeDtypeStruct(
            (3, columns, length) if out_planes else (columns, length), BF16
        ),
        cost_estimate=pl.CostEstimate(
            flops=2 * dots * columns * length * length,
            bytes_accessed=8 * columns * length * 2,
            transcendentals=heads * length * length,
        ),
    )(count, qkv, *grads)


def grad_partial_kernel(cot_ref, w0_ref, wy_ref, wc_ref, wcy_ref, all_ref, *out_refs):
    dp = lax.axis_index("dp")
    z, j = dp // 4, lax.rem(dp, 4)
    yl, c = j // 2, lax.rem(j, 2)
    for ref, flip_y, flip_c in ((w0_ref, 0, 0), (wy_ref, 1, 0), (wc_ref, 0, 1), (wcy_ref, 1, 1)):
        col = lax.rem(yl + flip_y, 2) * 2 + lax.rem(c + flip_c, 2)
        for k, apart in enumerate(APART):
            all_ref[z ^ apart, col] = ref[k]
    for (dx, dy), out_ref in zip(PLACES, out_refs):
        block = all_ref[tensor_place(dx, dy)].reshape(-1, all_ref.shape[3])
        out_ref[...] = dot(block, cot_ref[...], 0, 0).astype(BF16)


def grad_partial(cot, w0, wy, wc, wcy):
    columns, length = cot.shape
    rows = w0.shape[2]
    return pl.pallas_call(
        grad_partial_kernel,
        name="grad_partial",
        in_specs=[VMEM] * 5,
        out_specs=[VMEM] * 9,
        out_shape=[jax.ShapeDtypeStruct((Z, 4, columns // 4, rows), BF16)]
        + [jax.ShapeDtypeStruct((rows, length), BF16)] * 8,
        cost_estimate=pl.CostEstimate(
            flops=2 * 8 * columns * rows * length, bytes_accessed=8_000_000, transcendentals=0
        ),
    )(cot, w0, wy, wc, wcy)


def layer_out_kernel(flag_ref, all_ref, *refs):
    block_refs, (home_ref, guest_ref) = refs[:-2], refs[-2:]
    total = None
    for (dx, dy), block_ref in zip(PLACES, block_refs):
        weight = all_ref[tensor_place(dx, dy)].reshape(-1, all_ref.shape[3])
        term = dot(weight, block_ref[...], 1, 0)
        total = term if total is None else total + term
    sent = flag_ref[0] > 0
    home_ref[...] = jnp.where(sent, 0.0, total).astype(BF16)
    guest_ref[...] = jnp.where(sent, total, 0.0).astype(BF16)


def layer_out_of(flag, weight, blocks):
    rows, length = blocks[0].shape
    columns = 4 * weight.shape[2]
    return pl.pallas_call(
        layer_out_kernel,
        name="layer_out",
        in_specs=[SMEM, VMEM] + [VMEM] * 8,
        out_specs=[VMEM] * 2,
        out_shape=[jax.ShapeDtypeStruct((columns, length), BF16)] * 2,
        cost_estimate=pl.CostEstimate(
            flops=2 * 8 * columns * rows * length, bytes_accessed=6_000_000, transcendentals=0
        ),
    )(flag, weight, *blocks)


def weight_partial_kernel(cot_ref, *refs):
    block_refs, (keep_ref, send_ref, held) = refs[:-3], refs[-3:]
    dp = lax.axis_index("dp")
    z, j = dp // 4, lax.rem(dp, 4)
    yl, c = j // 2, lax.rem(j, 2)
    for (dx, dy), block_ref in zip(PLACES, block_refs):
        held[...] = dot(cot_ref[...], block_ref[...], 1, 1).astype(BF16).reshape(held.shape)
        apart = tensor_place(dx, dy) ^ z
        k = lax.rem(apart, 2) * 4 + lax.rem(apart // 2, 2) * 2 + apart // 4
        for out_ref, flip_c in ((keep_ref, 0), (send_ref, 1)):
            for flip_y in range(2):
                col = lax.rem(yl + flip_y, 2) * 2 + lax.rem(c + flip_c, 2)
                out_ref[flip_y, k] = held[col]


def weight_partial(cot, blocks):
    columns, length = cot.shape
    rows = blocks[0].shape[0]
    out = jax.ShapeDtypeStruct((2, Z, columns // 4, rows), BF16)
    return pl.pallas_call(
        weight_partial_kernel,
        name="weight_partial",
        in_specs=[VMEM] * 9,
        out_specs=[VMEM] * 2,
        out_shape=[out, out],
        scratch_shapes=[pltpu.VMEM((4, columns // 4, rows), BF16)],
        cost_estimate=pl.CostEstimate(
            flops=2 * 8 * columns * rows * length, bytes_accessed=6_000_000, transcendentals=0
        ),
    )(cot, *blocks)


def added(*terms):
    return functools.reduce(lambda a, b: a + b, [t.astype(F32) for t in terms]).astype(BF16)


def step(projected, residue_counts, migrate_plan, out_weight, out_cotangent):
    qkv = jnp.transpose(projected, (0, 2, 1))
    cot_slots = jnp.transpose(out_cotangent, (0, 2, 1))
    sent = migrate_plan[0] > 0

    moved = [swapped(out_weight.T, flip) for flip in (0, 4)]
    guest_cot = half_round(cot_slots[1])

    ctx = heads_call(forward_kernel, residue_counts, qkv, (), False)

    block = {(0, 0): ctx}
    block[0, 1] = along_tensor(ctx, 0, 1)
    block[2, 0] = along_tensor(ctx, 2, 0)
    block[-1, 0] = along_tensor(ctx, 1, 0)
    block[1, 0] = along_tensor(ctx, -1, 0)
    block[-1, 1] = along_tensor(block[0, 1], 1, 0)
    block[1, 1] = along_tensor(block[0, 1], -1, 0)
    block[2, 1] = along_tensor(block[2, 0], 0, 1)
    blocks = [block[place] for place in PLACES]

    stack = jnp.stack(moved)
    for bit in (2, 1):
        stack = jnp.concatenate([stack, exchanged(stack, 4 * bit)])
    w0 = stack
    wy = exchanged(w0, 2)
    wc = exchanged(w0, 1)
    wcy = exchanged(wy, 1)

    cot = jnp.where(sent, guest_cot, cot_slots[0])
    weight, *parts = grad_partial(cot, w0, wy, wc, wcy)
    part = dict(zip(PLACES, parts))

    from_other = along_tensor(part[2, 1], 0, 1)
    from_left = along_tensor(part[1, 1], 1, 0)
    from_right = along_tensor(part[-1, 1], -1, 0)
    got = [along_tensor(part[1, 0], 1, 0), along_tensor(part[-1, 0], -1, 0)]
    got.append(along_tensor(added(part[2, 0], from_other), 2, 0))
    got.append(along_tensor(added(part[0, 1], from_left, from_right), 0, 1))

    keep, send = weight_partial(cot, blocks)
    both = exchanged(send, 1)
    total = added(keep[0], both[0], exchanged(added(keep[1], both[1]), 2))
    for bit in (1, 2):
        half = total.shape[0] // 2
        total = added(total[:half], exchanged(total[half:], 4 * bit))
    sums = [swapped_back(total[i], flip) for i, flip in ((0, 0), (1, 4))]
    grad_weight = (sums[0].astype(F32) + sums[1].astype(F32)).T

    home, guest = layer_out_of(migrate_plan, weight, blocks)
    returned = half_round(guest)
    layer_out = jnp.transpose(jnp.stack([home, returned]), (0, 2, 1))

    grad_qkv = heads_call(backward_kernel, residue_counts, qkv, (part[0, 0], *got), True)
    return layer_out, jnp.transpose(grad_qkv, (0, 2, 1)), grad_weight


def solution(mesh):
    in_specs = (
        P(None, "dp", "tensor"),
        P("dp"),
        P("dp"),
        P("tensor", "dp"),
        P("dp", None, "tensor"),
    )
    out_specs = (P("dp", None, "tensor"), P(None, "dp", "tensor"), P("tensor", "dp"))
    return jax.shard_map(step, mesh=mesh, in_specs=in_specs, out_specs=out_specs, check_vma=False)
```

```python
import functools

import jax
import jax.numpy as jnp
from jax import lax
from jax.experimental import pallas as pl
from jax.experimental.pallas import tpu as pltpu
from jax.sharding import PartitionSpec as P


HEAD_DIM = 64
N_DP = 32
N_TENSOR = 8
X = N_TENSOR // 2
Z = N_DP // 4
BF16 = jnp.bfloat16
F32 = jnp.float32


SMEM = pl.BlockSpec(memory_space=pltpu.SMEM)
VMEM = pl.BlockSpec(memory_space=pltpu.VMEM)

PLACES = ((0, 0), (1, 0), (-1, 0), (2, 0), (0, 1), (1, 1), (-1, 1), (2, 1))

STEPS = (4, 3, 5, 2, 6, 1, 7, 0)


def dot(a, b, dim_a, dim_b):
    return lax.dot_general(a, b, (((dim_a,), (dim_b,)), ((), ())), preferred_element_type=F32)


def along_dp(value, to):
    return lax.ppermute(value, "dp", [(i, to(i)) for i in range(N_DP)])


def along_tensor(value, dx, dy):
    def to(i):
        return ((i // 2 + dx) % X) * 2 + ((i % 2) ^ dy)

    return lax.ppermute(value, "tensor", [(i, to(i)) for i in range(N_TENSOR)])


def swap_pairs():
    pairs = []
    for t in range(N_TENSOR):
        for j in range(4):
            for (dx, dy), steps in zip(PLACES, STEPS):
                rows = ((t // 2 + dx) % X) * 2 + ((t % 2) ^ dy)
                home = (4 * t + j) * N_TENSOR + rows
                pairs.append((home, (4 * ((t + steps) % Z) + j) * N_TENSOR + t))
    return pairs


def swapped(value, pairs):
    return lax.ppermute(value, ("dp", "tensor"), pairs)


def exchanged(value, flip):
    return along_dp(value, lambda i: i ^ flip)


def half_round(value):
    return along_dp(value, lambda i: (i + N_DP // 2) % N_DP)


def stack_index(steps):
    z = lax.axis_index("dp") // 4
    apart = lax.rem(lax.axis_index("tensor") + steps, Z) ^ z
    return lax.rem(apart, 2) * 4 + lax.rem(apart // 2, 2) * 2 + apart // 4


def column_of(flip_y, flip_c):
    j = lax.rem(lax.axis_index("dp"), 4)
    return lax.rem(j // 2 + flip_y, 2) * 2 + lax.rem(j + flip_c, 2)


def probs_of(q, k, count):
    scores = dot(k, q, 0, 0)
    rows = lax.broadcasted_iota(jnp.int32, scores.shape, 0)
    scores = jnp.where(rows < count, scores, -1000000000.0)
    exponent = jnp.exp(scores - jnp.max(scores, axis=0, keepdims=True))
    return exponent * (1.0 / jnp.sum(exponent, axis=0, keepdims=True))


def forward_kernel(count_ref, qkv_ref, ctx_ref):
    count = count_ref[0]
    live = lax.broadcasted_iota(jnp.int32, (1, ctx_ref.shape[1]), 1) < count
    q = qkv_ref[0] * jnp.asarray(HEAD_DIM ** (-0.5), BF16)
    probs = probs_of(q, qkv_ref[1], count).astype(BF16)
    context = dot(qkv_ref[2], probs, 1, 0)
    ctx_ref[...] = jnp.where(live, context, 0.0).astype(BF16)


def backward_kernel(count_ref, qkv_ref, *refs):
    grad_refs, out_ref = refs[:-1], refs[-1]
    count = count_ref[0]
    grad = functools.reduce(lambda a, b: a + b, [r[...].astype(F32) for r in grad_refs])
    live = lax.broadcasted_iota(jnp.int32, (1, grad.shape[1]), 1) < count
    grad = jnp.where(live, grad, 0.0).astype(BF16)
    scale = jnp.asarray(HEAD_DIM ** (-0.5), BF16)
    q, k, v = qkv_ref[0] * scale, qkv_ref[1], qkv_ref[2]
    probs = probs_of(q, k, count)
    out_ref[2] = dot(grad, probs.astype(BF16), 1, 1).astype(BF16)
    grad_probs = dot(v, grad, 0, 0).astype(BF16).astype(F32)
    inner = jnp.sum(probs * grad_probs, axis=0, keepdims=True)
    grad_scores = (probs * (grad_probs - inner)).astype(BF16)
    out_ref[0] = (dot(k, grad_scores, 1, 0) * HEAD_DIM ** (-0.5)).astype(BF16)
    out_ref[1] = dot(q, grad_scores, 1, 1).astype(BF16)


def heads_call(kernel, count, qkv, grads, out_planes):
    _, columns, length = qkv.shape
    heads = columns // HEAD_DIM
    plane = pl.BlockSpec((HEAD_DIM, length), lambda h: (h, 0))
    planes = pl.BlockSpec((3, HEAD_DIM, length), lambda h: (0, h, 0))
    dots = 6 if out_planes else 2
    return pl.pallas_call(
        kernel,
        grid=(heads,),
        in_specs=[SMEM, planes] + [plane] * len(grads),
        out_specs=planes if out_planes else plane,
        out_shape=jax.ShapeDtypeStruct(
            (3, columns, length) if out_planes else (columns, length), BF16
        ),
        compiler_params=pltpu.CompilerParams(vmem_limit_bytes=16 << 20),
        cost_estimate=pl.CostEstimate(
            flops=2 * dots * columns * length * length,
            bytes_accessed=8 * columns * length * 2,
            transcendentals=heads * length * length,
        ),
    )(count, qkv, *grads)


def grad_partial_kernel(cot_ref, w0_ref, wy_ref, wc_ref, wcy_ref, all_ref, *out_refs):
    for place, (steps, out_ref) in enumerate(zip(STEPS, out_refs)):
        k = stack_index(steps)
        all_ref[place, column_of(0, 0)] = w0_ref[k]
        all_ref[place, column_of(1, 0)] = wy_ref[k]
        all_ref[place, column_of(0, 1)] = wc_ref[k]
        all_ref[place, column_of(1, 1)] = wcy_ref[k]
        block = all_ref[place].reshape(-1, all_ref.shape[3])
        out_ref[...] = dot(block, cot_ref[...], 0, 0).astype(BF16)


def grad_partial(cot, w0, wy, wc, wcy):
    columns, length = cot.shape
    rows = w0.shape[2]
    return pl.pallas_call(
        grad_partial_kernel,
        name="grad_partial",
        in_specs=[VMEM] * 5,
        out_specs=[VMEM] * 9,
        out_shape=[jax.ShapeDtypeStruct((Z, 4, columns // 4, rows), BF16)]
        + [jax.ShapeDtypeStruct((rows, length), BF16)] * 8,
        compiler_params=pltpu.CompilerParams(vmem_limit_bytes=16 << 20),
        cost_estimate=pl.CostEstimate(
            flops=2 * 8 * columns * rows * length, bytes_accessed=8_000_000, transcendentals=0
        ),
    )(cot, w0, wy, wc, wcy)


def layer_out_kernel(flag_ref, all_ref, *refs):
    block_refs, (home_ref, guest_ref) = refs[:-2], refs[-2:]
    total = None
    for place, block_ref in enumerate(block_refs):
        weight = all_ref[place].reshape(-1, all_ref.shape[3])
        term = dot(weight, block_ref[...], 1, 0)
        total = term if total is None else total + term
    sent = flag_ref[0] > 0
    home_ref[...] = jnp.where(sent, 0.0, total).astype(BF16)
    guest_ref[...] = jnp.where(sent, total, 0.0).astype(BF16)


def layer_out_of(flag, weight, blocks):
    rows, length = blocks[0].shape
    columns = 4 * weight.shape[2]
    return pl.pallas_call(
        layer_out_kernel,
        name="layer_out",
        in_specs=[SMEM, VMEM] + [VMEM] * 8,
        out_specs=[VMEM] * 2,
        out_shape=[jax.ShapeDtypeStruct((columns, length), BF16)] * 2,
        compiler_params=pltpu.CompilerParams(vmem_limit_bytes=16 << 20),
        cost_estimate=pl.CostEstimate(
            flops=2 * 8 * columns * rows * length, bytes_accessed=6_000_000, transcendentals=0
        ),
    )(flag, weight, *blocks)


def weight_partial_kernel(cot_ref, *refs):
    block_refs, (keep_ref, send_ref, held) = refs[:-3], refs[-3:]
    for steps, block_ref in zip(STEPS, block_refs):
        held[...] = dot(cot_ref[...], block_ref[...], 1, 1).astype(BF16).reshape(held.shape)
        k = stack_index(steps)
        for flip_y in range(2):
            keep_ref[flip_y, k] = held[column_of(flip_y, 0)]
            send_ref[flip_y, k] = held[column_of(flip_y, 1)]


def weight_partial(cot, blocks):
    columns, length = cot.shape
    rows = blocks[0].shape[0]
    out = jax.ShapeDtypeStruct((2, Z, columns // 4, rows), BF16)
    return pl.pallas_call(
        weight_partial_kernel,
        name="weight_partial",
        in_specs=[VMEM] * 9,
        out_specs=[VMEM] * 2,
        out_shape=[out, out],
        scratch_shapes=[pltpu.VMEM((4, columns // 4, rows), BF16)],
        compiler_params=pltpu.CompilerParams(vmem_limit_bytes=16 << 20),
        cost_estimate=pl.CostEstimate(
            flops=2 * 8 * columns * rows * length, bytes_accessed=6_000_000, transcendentals=0
        ),
    )(cot, *blocks)


def added(*terms):
    return functools.reduce(lambda a, b: a + b, [t.astype(F32) for t in terms]).astype(BF16)


def step(projected, residue_counts, migrate_plan, out_weight, out_cotangent):
    qkv = jnp.transpose(projected, (0, 2, 1))
    cot_slots = jnp.transpose(out_cotangent, (0, 2, 1))
    sent = migrate_plan[0] > 0

    pairs = swap_pairs()
    moved = swapped(out_weight.T, pairs)
    guest_cot = half_round(cot_slots[1])

    ctx = heads_call(forward_kernel, residue_counts, qkv, (), False)

    block = {(0, 0): ctx}
    block[0, 1] = along_tensor(ctx, 0, 1)
    block[2, 0] = along_tensor(ctx, 2, 0)
    block[-1, 0] = along_tensor(ctx, 1, 0)
    block[1, 0] = along_tensor(ctx, -1, 0)
    block[-1, 1] = along_tensor(block[0, 1], 1, 0)
    block[1, 1] = along_tensor(block[0, 1], -1, 0)
    block[2, 1] = along_tensor(block[2, 0], 0, 1)
    blocks = [block[place] for place in PLACES]

    stack = moved[None]
    for bit in (4, 2, 1):
        stack = jnp.concatenate([stack, exchanged(stack, 4 * bit)])
    w0 = stack
    wy = exchanged(w0, 2)
    wc = exchanged(w0, 1)
    wcy = exchanged(wy, 1)

    cot = jnp.where(sent, guest_cot, cot_slots[0])
    weight, *parts = grad_partial(cot, w0, wy, wc, wcy)
    part = dict(zip(PLACES, parts))

    from_other = along_tensor(part[2, 1], 0, 1)
    from_left = along_tensor(part[1, 1], 1, 0)
    from_right = along_tensor(part[-1, 1], -1, 0)
    got = [along_tensor(part[1, 0], 1, 0), along_tensor(part[-1, 0], -1, 0)]
    got.append(along_tensor(added(part[2, 0], from_other), 2, 0))
    got.append(along_tensor(added(part[0, 1], from_left, from_right), 0, 1))

    keep, send = weight_partial(cot, blocks)
    both = exchanged(send, 1)
    total = added(keep[0], both[0], exchanged(added(keep[1], both[1]), 2))
    for bit in (1, 2, 4):
        half = total.shape[0] // 2
        total = added(total[:half], exchanged(total[half:], 4 * bit))
    home_pairs = [(there, here) for here, there in pairs]
    grad_weight = swapped(total[0], home_pairs).astype(F32).T

    home, guest = layer_out_of(migrate_plan, weight, blocks)
    returned = half_round(guest)
    layer_out = jnp.transpose(jnp.stack([home, returned]), (0, 2, 1))

    grad_qkv = heads_call(backward_kernel, residue_counts, qkv, (part[0, 0], *got), True)
    return layer_out, jnp.transpose(grad_qkv, (0, 2, 1)), grad_weight


def solution(mesh):
    in_specs = (
        P(None, "dp", "tensor"),
        P("dp"),
        P("dp"),
        P("tensor", "dp"),
        P("dp", None, "tensor"),
    )
    out_specs = (P("dp", None, "tensor"), P(None, "dp", "tensor"), P("tensor", "dp"))
    return jax.shard_map(step, mesh=mesh, in_specs=in_specs, out_specs=out_specs, check_vma=False)
```

```python
import functools

import jax
import jax.numpy as jnp
from jax import lax
from jax.experimental import pallas as pl
from jax.experimental.pallas import tpu as pltpu
from jax.sharding import PartitionSpec as P


HEAD_DIM = 64
N_DP = 32
N_TENSOR = 8
X = N_TENSOR // 2
Z = N_DP // 4
BF16 = jnp.bfloat16
F32 = jnp.float32


SMEM = pl.BlockSpec(memory_space=pltpu.SMEM)
VMEM = pl.BlockSpec(memory_space=pltpu.VMEM)

PLACES = ((0, 0), (1, 0), (-1, 0), (2, 0), (0, 1), (1, 1), (-1, 1), (2, 1))

STEPS = (4, 3, 5, 2, 6, 1, 7, 0)


def dot(a, b, dim_a, dim_b):
    return lax.dot_general(a, b, (((dim_a,), (dim_b,)), ((), ())), preferred_element_type=F32)


def along_dp(value, to):
    return lax.ppermute(value, "dp", [(i, to(i)) for i in range(N_DP)])


def along_tensor(value, dx, dy):
    def to(i):
        return ((i // 2 + dx) % X) * 2 + ((i % 2) ^ dy)

    return lax.ppermute(value, "tensor", [(i, to(i)) for i in range(N_TENSOR)])


def swap_pairs():
    pairs = []
    for t in range(N_TENSOR):
        for j in range(4):
            for (dx, dy), steps in zip(PLACES, STEPS):
                rows = ((t // 2 + dx) % X) * 2 + ((t % 2) ^ dy)
                home = (4 * t + j) * N_TENSOR + rows
                pairs.append((home, (4 * ((t + steps) % Z) + j) * N_TENSOR + t))
    return pairs


def swapped(value, pairs):
    return lax.ppermute(value, ("dp", "tensor"), pairs)


def exchanged(value, flip):
    return along_dp(value, lambda i: i ^ flip)


def half_round(value):
    return along_dp(value, lambda i: (i + N_DP // 2) % N_DP)


def stack_index(steps):
    z = lax.axis_index("dp") // 4
    apart = lax.rem(lax.axis_index("tensor") + steps, Z) ^ z
    return lax.rem(apart, 4) * 2 + apart // 4


def column_of(flip_y, flip_c):
    j = lax.rem(lax.axis_index("dp"), 4)
    return lax.rem(j // 2 + flip_y, 2) * 2 + lax.rem(j + flip_c, 2)


def probs_of(q, k, count):
    scores = dot(k, q, 0, 0)
    rows = lax.broadcasted_iota(jnp.int32, scores.shape, 0)
    scores = jnp.where(rows < count, scores, -1000000000.0)
    exponent = jnp.exp(scores - jnp.max(scores, axis=0, keepdims=True))
    return exponent * (1.0 / jnp.sum(exponent, axis=0, keepdims=True))


def forward_kernel(count_ref, qkv_ref, ctx_ref):
    count = count_ref[0]
    live = lax.broadcasted_iota(jnp.int32, (1, ctx_ref.shape[1]), 1) < count
    q = qkv_ref[0] * jnp.asarray(HEAD_DIM ** (-0.5), BF16)
    probs = probs_of(q, qkv_ref[1], count).astype(BF16)
    context = dot(qkv_ref[2], probs, 1, 0)
    ctx_ref[...] = jnp.where(live, context, 0.0).astype(BF16)


def backward_kernel(skipped, count_ref, *refs):
    qkv_ref, grad_refs, out_ref = refs[skipped], refs[skipped + 1 : -1], refs[-1]
    count = count_ref[0]
    grad = functools.reduce(lambda a, b: a + b, [r[...].astype(F32) for r in grad_refs])
    live = lax.broadcasted_iota(jnp.int32, (1, grad.shape[1]), 1) < count
    grad = jnp.where(live, grad, 0.0).astype(BF16)
    scale = jnp.asarray(HEAD_DIM ** (-0.5), BF16)
    q, k, v = qkv_ref[0] * scale, qkv_ref[1], qkv_ref[2]
    probs = probs_of(q, k, count)
    out_ref[2] = dot(grad, probs.astype(BF16), 1, 1).astype(BF16)
    grad_probs = dot(v, grad, 0, 0).astype(BF16).astype(F32)
    inner = jnp.sum(probs * grad_probs, axis=0, keepdims=True)
    grad_scores = (probs * (grad_probs - inner)).astype(BF16)
    out_ref[0] = (dot(k, grad_scores, 1, 0) * HEAD_DIM ** (-0.5)).astype(BF16)
    out_ref[1] = dot(q, grad_scores, 1, 1).astype(BF16)


def kernel_cost(dots, heads, length):
    return pl.CostEstimate(
        flops=2 * dots * heads * HEAD_DIM * length * length,
        bytes_accessed=8 * heads * HEAD_DIM * length * 2,
        transcendentals=heads * length * length,
    )


def forward(count, qkv):
    _, columns, length = qkv.shape
    heads = columns // HEAD_DIM
    return pl.pallas_call(
        forward_kernel,
        name="forward",
        grid=(heads,),
        in_specs=[SMEM, pl.BlockSpec((3, HEAD_DIM, length), lambda h: (0, h, 0))],
        out_specs=pl.BlockSpec((HEAD_DIM, length), lambda h: (h, 0)),
        out_shape=jax.ShapeDtypeStruct((columns, length), BF16),
        compiler_params=pltpu.CompilerParams(vmem_limit_bytes=16 << 20),
        cost_estimate=kernel_cost(2, heads, length),
    )(count, qkv)


def backward(count, qkv, grads, first, heads, earlier=None):
    length = qkv.shape[2]
    plane = pl.BlockSpec((HEAD_DIM, length), lambda h: (h + first, 0))
    planes = pl.BlockSpec((3, HEAD_DIM, length), lambda h: (0, h + first, 0))
    before = [] if earlier is None else [earlier]
    return pl.pallas_call(
        functools.partial(backward_kernel, len(before)),
        name="backward",
        grid=(heads,),
        in_specs=[SMEM]
        + [pl.BlockSpec(memory_space=pl.ANY)] * len(before)
        + [planes]
        + [plane] * len(grads),
        out_specs=planes,
        out_shape=jax.ShapeDtypeStruct(qkv.shape, BF16),
        input_output_aliases={1: 0} if before else {},
        compiler_params=pltpu.CompilerParams(vmem_limit_bytes=16 << 20),
        cost_estimate=kernel_cost(6, heads, length),
    )(count, *before, qkv, *grads)


def grad_partial_kernel(cot_ref, w0_ref, wy_ref, wc_ref, wcy_ref, all_ref, *out_refs):
    for place, (steps, out_ref) in enumerate(zip(STEPS, out_refs)):
        k = stack_index(steps)
        all_ref[place, column_of(0, 0)] = w0_ref[k]
        all_ref[place, column_of(1, 0)] = wy_ref[k]
        all_ref[place, column_of(0, 1)] = wc_ref[k]
        all_ref[place, column_of(1, 1)] = wcy_ref[k]
        block = all_ref[place].reshape(-1, all_ref.shape[3])
        out_ref[...] = dot(block, cot_ref[...], 0, 0).astype(BF16)


def grad_partial(cot, w0, wy, wc, wcy):
    columns, length = cot.shape
    rows = w0.shape[2]
    return pl.pallas_call(
        grad_partial_kernel,
        name="grad_partial",
        in_specs=[VMEM] * 5,
        out_specs=[VMEM] * 9,
        out_shape=[jax.ShapeDtypeStruct((Z, 4, columns // 4, rows), BF16)]
        + [jax.ShapeDtypeStruct((rows, length), BF16)] * 8,
        compiler_params=pltpu.CompilerParams(vmem_limit_bytes=16 << 20),
        cost_estimate=pl.CostEstimate(
            flops=2 * 8 * columns * rows * length, bytes_accessed=8_000_000, transcendentals=0
        ),
    )(cot, w0, wy, wc, wcy)


def layer_out_kernel(flag_ref, all_ref, *refs):
    block_refs, (home_ref, guest_ref) = refs[:-2], refs[-2:]
    total = None
    for place, block_ref in enumerate(block_refs):
        weight = all_ref[place].reshape(-1, all_ref.shape[3])
        term = dot(weight, block_ref[...], 1, 0)
        total = term if total is None else total + term
    sent = flag_ref[0] > 0
    home_ref[...] = jnp.where(sent, 0.0, total).astype(BF16)
    guest_ref[...] = jnp.where(sent, total, 0.0).astype(BF16)


def layer_out_of(flag, weight, blocks):
    rows, length = blocks[0].shape
    columns = 4 * weight.shape[2]
    return pl.pallas_call(
        layer_out_kernel,
        name="layer_out",
        in_specs=[SMEM, VMEM] + [VMEM] * 8,
        out_specs=[VMEM] * 2,
        out_shape=[jax.ShapeDtypeStruct((columns, length), BF16)] * 2,
        compiler_params=pltpu.CompilerParams(vmem_limit_bytes=16 << 20),
        cost_estimate=pl.CostEstimate(
            flops=2 * 8 * columns * rows * length, bytes_accessed=6_000_000, transcendentals=0
        ),
    )(flag, weight, *blocks)


def weight_partial_kernel(cot_ref, *refs):
    block_refs, (keep_ref, send_ref, held) = refs[:-3], refs[-3:]
    for steps, block_ref in zip(STEPS, block_refs):
        held[...] = dot(cot_ref[...], block_ref[...], 1, 1).astype(BF16).reshape(held.shape)
        k = stack_index(steps)
        for flip_y in range(2):
            keep_ref[flip_y, k] = held[column_of(flip_y, 0)]
            send_ref[flip_y, k] = held[column_of(flip_y, 1)]


def weight_partial(cot, blocks):
    columns, length = cot.shape
    rows = blocks[0].shape[0]
    out = jax.ShapeDtypeStruct((2, Z, columns // 4, rows), BF16)
    return pl.pallas_call(
        weight_partial_kernel,
        name="weight_partial",
        in_specs=[VMEM] * 9,
        out_specs=[VMEM] * 2,
        out_shape=[out, out],
        scratch_shapes=[pltpu.VMEM((4, columns // 4, rows), BF16)],
        compiler_params=pltpu.CompilerParams(vmem_limit_bytes=16 << 20),
        cost_estimate=pl.CostEstimate(
            flops=2 * 8 * columns * rows * length, bytes_accessed=6_000_000, transcendentals=0
        ),
    )(cot, *blocks)


def added(*terms):
    return functools.reduce(lambda a, b: a + b, [t.astype(F32) for t in terms]).astype(BF16)


def step(projected, residue_counts, migrate_plan, out_weight, out_cotangent):
    qkv = jnp.transpose(projected, (0, 2, 1))
    cot_slots = jnp.transpose(out_cotangent, (0, 2, 1))
    sent = migrate_plan[0] > 0

    pairs = swap_pairs()
    moved = swapped(out_weight.T, pairs)

    ctx = forward(residue_counts, qkv)

    cot_slots, ctx = lax.optimization_barrier((cot_slots, ctx))
    guest_cot = half_round(cot_slots[1])

    block = {(0, 0): ctx}
    block[0, 1] = along_tensor(ctx, 0, 1)
    block[2, 0] = along_tensor(ctx, 2, 0)
    block[-1, 0] = along_tensor(ctx, 1, 0)
    block[1, 0] = along_tensor(ctx, -1, 0)
    block[-1, 1] = along_tensor(block[0, 1], 1, 0)
    block[1, 1] = along_tensor(block[0, 1], -1, 0)
    block[2, 1] = along_tensor(block[2, 0], 0, 1)
    blocks = [block[place] for place in PLACES]

    two = jnp.stack([moved, exchanged(moved, 16)])
    w0 = jnp.concatenate([two] + [exchanged(two, 4 * far) for far in (1, 2, 3)])
    wy = exchanged(w0, 2)
    wc = exchanged(w0, 1)
    wcy = exchanged(wy, 1)

    cot = jnp.where(sent, guest_cot, cot_slots[0])
    weight, *parts = grad_partial(cot, w0, wy, wc, wcy)
    part = dict(zip(PLACES, parts))

    from_other = along_tensor(part[2, 1], 0, 1)
    from_left = along_tensor(part[1, 1], 1, 0)
    from_right = along_tensor(part[-1, 1], -1, 0)
    got = [along_tensor(part[1, 0], 1, 0), along_tensor(part[-1, 0], -1, 0)]
    got.append(along_tensor(added(part[2, 0], from_other), 2, 0))
    got.append(along_tensor(added(part[0, 1], from_left, from_right), 0, 1))

    keep, send = weight_partial(cot, blocks)
    both = exchanged(send, 1)
    total = added(keep[0], both[0], exchanged(added(keep[1], both[1]), 2))
    terms = [exchanged(total[2 * far : 2 * far + 2], 4 * far) for far in (1, 2, 3)]
    total = added(total[:2], *terms)
    total = added(total[0], exchanged(total[1], 16))
    home_pairs = [(there, here) for here, there in pairs]
    grad_weight = swapped(total, home_pairs).astype(F32).T

    home, guest = layer_out_of(migrate_plan, weight, blocks)
    returned = half_round(guest)
    layer_out = jnp.transpose(jnp.stack([home, returned]), (0, 2, 1))

    grads = (part[0, 0], *got)
    heads = qkv.shape[1] // HEAD_DIM
    early = heads - heads // 2
    grad_qkv = backward(residue_counts, qkv, grads, 0, early)
    grad_qkv = backward(residue_counts, qkv, grads, early, heads - early, grad_qkv)
    return layer_out, jnp.transpose(grad_qkv, (0, 2, 1)), grad_weight


def solution(mesh):
    in_specs = (
        P(None, "dp", "tensor"),
        P("dp"),
        P("dp"),
        P("tensor", "dp"),
        P("dp", None, "tensor"),
    )
    out_specs = (P("dp", None, "tensor"), P(None, "dp", "tensor"), P("tensor", "dp"))
    return jax.shard_map(step, mesh=mesh, in_specs=in_specs, out_specs=out_specs, check_vma=False)
```

```python
import functools

import jax
import jax.numpy as jnp
from jax import lax
from jax.experimental import pallas as pl
from jax.experimental.pallas import tpu as pltpu
from jax.sharding import PartitionSpec as P


HEAD_DIM = 64
N_DP = 32
N_TENSOR = 8
X = N_TENSOR // 2
Z = N_DP // 4
BF16 = jnp.bfloat16
F32 = jnp.float32


SMEM = pl.BlockSpec(memory_space=pltpu.SMEM)
VMEM = pl.BlockSpec(memory_space=pltpu.VMEM)

PLACES = ((0, 0), (1, 0), (-1, 0), (2, 0), (0, 1), (1, 1), (-1, 1), (2, 1))

STEPS = (4, 3, 5, 2, 6, 1, 7, 0)


def dot(a, b, dim_a, dim_b):
    return lax.dot_general(a, b, (((dim_a,), (dim_b,)), ((), ())), preferred_element_type=F32)


def along_dp(value, to):
    return lax.ppermute(value, "dp", [(i, to(i)) for i in range(N_DP)])


def along_tensor(value, dx, dy):
    def to(i):
        return ((i // 2 + dx) % X) * 2 + ((i % 2) ^ dy)

    return lax.ppermute(value, "tensor", [(i, to(i)) for i in range(N_TENSOR)])


def swap_pairs():
    pairs = []
    for t in range(N_TENSOR):
        for j in range(4):
            for (dx, dy), steps in zip(PLACES, STEPS):
                rows = ((t // 2 + dx) % X) * 2 + ((t % 2) ^ dy)
                home = (4 * t + j) * N_TENSOR + rows
                pairs.append((home, (4 * ((t + steps) % Z) + j) * N_TENSOR + t))
    return pairs


def swapped(value, pairs):
    return lax.ppermute(value, ("dp", "tensor"), pairs)


def exchanged(value, flip):
    return along_dp(value, lambda i: i ^ flip)


def half_round(value):
    return along_dp(value, lambda i: (i + N_DP // 2) % N_DP)


def stack_index(steps):
    z = lax.axis_index("dp") // 4
    apart = lax.rem(lax.axis_index("tensor") + steps, Z) ^ z
    return lax.rem(apart, 4) * 2 + apart // 4


def column_of(flip_y, flip_c):
    j = lax.rem(lax.axis_index("dp"), 4)
    return lax.rem(j // 2 + flip_y, 2) * 2 + lax.rem(j + flip_c, 2)


def probs_of(q, k, count):
    scores = dot(k, q, 0, 0)
    rows = lax.broadcasted_iota(jnp.int32, scores.shape, 0)
    scores = jnp.where(rows < count, scores, -1000000000.0)
    exponent = jnp.exp(scores - jnp.max(scores, axis=0, keepdims=True))
    return exponent * (1.0 / jnp.sum(exponent, axis=0, keepdims=True))


def forward_kernel(count_ref, qkv_ref, ctx_ref):
    count = count_ref[0]
    live = lax.broadcasted_iota(jnp.int32, (1, ctx_ref.shape[1]), 1) < count
    q = qkv_ref[0] * jnp.asarray(HEAD_DIM ** (-0.5), BF16)
    probs = probs_of(q, qkv_ref[1], count).astype(BF16)
    context = dot(qkv_ref[2], probs, 1, 0)
    ctx_ref[...] = jnp.where(live, context, 0.0).astype(BF16)


def backward_kernel(count_ref, qkv_ref, *refs):
    grad_refs, out_ref = refs[:-1], refs[-1]
    count = count_ref[0]
    grad = functools.reduce(lambda a, b: a + b, [r[...].astype(F32) for r in grad_refs])
    live = lax.broadcasted_iota(jnp.int32, (1, grad.shape[1]), 1) < count
    grad = jnp.where(live, grad, 0.0).astype(BF16)
    scale = jnp.asarray(HEAD_DIM ** (-0.5), BF16)
    q, k, v = qkv_ref[0] * scale, qkv_ref[1], qkv_ref[2]
    probs = probs_of(q, k, count)
    out_ref[2] = dot(grad, probs.astype(BF16), 1, 1).astype(BF16)
    grad_probs = dot(v, grad, 0, 0).astype(BF16).astype(F32)
    inner = jnp.sum(probs * grad_probs, axis=0, keepdims=True)
    grad_scores = (probs * (grad_probs - inner)).astype(BF16)
    out_ref[0] = (dot(k, grad_scores, 1, 0) * HEAD_DIM ** (-0.5)).astype(BF16)
    out_ref[1] = dot(q, grad_scores, 1, 1).astype(BF16)


def kernel_cost(dots, heads, length):
    return pl.CostEstimate(
        flops=2 * dots * heads * HEAD_DIM * length * length,
        bytes_accessed=8 * heads * HEAD_DIM * length * 2,
        transcendentals=heads * length * length,
    )


def forward(count, qkv):
    _, columns, length = qkv.shape
    heads = columns // HEAD_DIM
    return pl.pallas_call(
        forward_kernel,
        name="forward",
        grid=(heads,),
        in_specs=[SMEM, pl.BlockSpec((3, HEAD_DIM, length), lambda h: (0, h, 0))],
        out_specs=pl.BlockSpec((HEAD_DIM, length), lambda h: (h, 0)),
        out_shape=jax.ShapeDtypeStruct((columns, length), BF16),
        compiler_params=pltpu.CompilerParams(vmem_limit_bytes=16 << 20),
        cost_estimate=kernel_cost(2, heads, length),
    )(count, qkv)


def backward(count, qkv, grads):
    _, columns, length = qkv.shape
    heads = columns // HEAD_DIM
    plane = pl.BlockSpec((HEAD_DIM, length), lambda h: (h, 0))
    planes = pl.BlockSpec((3, HEAD_DIM, length), lambda h: (0, h, 0))
    return pl.pallas_call(
        backward_kernel,
        name="backward",
        grid=(heads,),
        in_specs=[SMEM, planes] + [plane] * len(grads),
        out_specs=planes,
        out_shape=jax.ShapeDtypeStruct(qkv.shape, BF16),
        compiler_params=pltpu.CompilerParams(vmem_limit_bytes=16 << 20),
        cost_estimate=kernel_cost(6, heads, length),
    )(count, qkv, *grads)


def grad_partial_kernel(cot_ref, w0_ref, wy_ref, wc_ref, wcy_ref, all_ref, *out_refs):
    for place, (steps, out_ref) in enumerate(zip(STEPS, out_refs)):
        k = stack_index(steps)
        all_ref[place, column_of(0, 0)] = w0_ref[k]
        all_ref[place, column_of(1, 0)] = wy_ref[k]
        all_ref[place, column_of(0, 1)] = wc_ref[k]
        all_ref[place, column_of(1, 1)] = wcy_ref[k]
        block = all_ref[place].reshape(-1, all_ref.shape[3])
        out_ref[...] = dot(block, cot_ref[...], 0, 0).astype(BF16)


def grad_partial(cot, w0, wy, wc, wcy):
    columns, length = cot.shape
    rows = w0.shape[2]
    return pl.pallas_call(
        grad_partial_kernel,
        name="grad_partial",
        in_specs=[VMEM] * 5,
        out_specs=[VMEM] * 9,
        out_shape=[jax.ShapeDtypeStruct((Z, 4, columns // 4, rows), BF16)]
        + [jax.ShapeDtypeStruct((rows, length), BF16)] * 8,
        compiler_params=pltpu.CompilerParams(vmem_limit_bytes=16 << 20),
        cost_estimate=pl.CostEstimate(
            flops=2 * 8 * columns * rows * length, bytes_accessed=8_000_000, transcendentals=0
        ),
    )(cot, w0, wy, wc, wcy)


def layer_out_kernel(flag_ref, all_ref, *refs):
    block_refs, (home_ref, guest_ref) = refs[:-2], refs[-2:]
    total = None
    for place, block_ref in enumerate(block_refs):
        weight = all_ref[place].reshape(-1, all_ref.shape[3])
        term = dot(weight, block_ref[...], 1, 0)
        total = term if total is None else total + term
    sent = flag_ref[0] > 0
    home_ref[...] = jnp.where(sent, 0.0, total).astype(BF16)
    guest_ref[...] = jnp.where(sent, total, 0.0).astype(BF16)


def layer_out_of(flag, weight, blocks):
    rows, length = blocks[0].shape
    columns = 4 * weight.shape[2]
    return pl.pallas_call(
        layer_out_kernel,
        name="layer_out",
        in_specs=[SMEM, VMEM] + [VMEM] * 8,
        out_specs=[VMEM] * 2,
        out_shape=[jax.ShapeDtypeStruct((columns, length), BF16)] * 2,
        compiler_params=pltpu.CompilerParams(vmem_limit_bytes=16 << 20),
        cost_estimate=pl.CostEstimate(
            flops=2 * 8 * columns * rows * length, bytes_accessed=6_000_000, transcendentals=0
        ),
    )(flag, weight, *blocks)


def weight_partial_kernel(cot_ref, *refs):
    block_refs, (keep_ref, send_ref, held) = refs[:-3], refs[-3:]
    for steps, block_ref in zip(STEPS, block_refs):
        held[...] = dot(cot_ref[...], block_ref[...], 1, 1).astype(BF16).reshape(held.shape)
        k = stack_index(steps)
        for flip_y in range(2):
            keep_ref[flip_y, k] = held[column_of(flip_y, 0)]
            send_ref[flip_y, k] = held[column_of(flip_y, 1)]


def weight_partial(cot, blocks):
    columns, length = cot.shape
    rows = blocks[0].shape[0]
    out = jax.ShapeDtypeStruct((2, Z, columns // 4, rows), BF16)
    return pl.pallas_call(
        weight_partial_kernel,
        name="weight_partial",
        in_specs=[VMEM] * 9,
        out_specs=[VMEM] * 2,
        out_shape=[out, out],
        scratch_shapes=[pltpu.VMEM((4, columns // 4, rows), BF16)],
        compiler_params=pltpu.CompilerParams(vmem_limit_bytes=16 << 20),
        cost_estimate=pl.CostEstimate(
            flops=2 * 8 * columns * rows * length, bytes_accessed=6_000_000, transcendentals=0
        ),
    )(cot, *blocks)


def added(*terms):
    return functools.reduce(lambda a, b: a + b, [t.astype(F32) for t in terms]).astype(BF16)


def step(projected, residue_counts, migrate_plan, out_weight, out_cotangent):
    qkv = jnp.transpose(projected, (0, 2, 1))
    cot_slots = jnp.transpose(out_cotangent, (0, 2, 1))
    sent = migrate_plan[0] > 0

    pairs = swap_pairs()
    moved = swapped(out_weight.T, pairs)

    ctx = forward(residue_counts, qkv)

    cot_slots, ctx = lax.optimization_barrier((cot_slots, ctx))
    guest_cot = half_round(cot_slots[1])

    block = {(0, 0): ctx}
    block[0, 1] = along_tensor(ctx, 0, 1)
    block[2, 0] = along_tensor(ctx, 2, 0)
    block[-1, 0] = along_tensor(ctx, 1, 0)
    block[1, 0] = along_tensor(ctx, -1, 0)
    block[-1, 1] = along_tensor(block[0, 1], 1, 0)
    block[1, 1] = along_tensor(block[0, 1], -1, 0)
    block[2, 1] = along_tensor(block[0, 1], 2, 0)
    blocks = [block[place] for place in PLACES]

    two = jnp.stack([moved, exchanged(moved, 16)])
    w0 = jnp.concatenate([two] + [exchanged(two, 4 * far) for far in (1, 2, 3)])
    wy = exchanged(w0, 2)
    wc = exchanged(w0, 1)
    wcy = exchanged(wy, 1)

    cot = jnp.where(sent, guest_cot, cot_slots[0])
    weight, *parts = grad_partial(cot, w0, wy, wc, wcy)
    part = dict(zip(PLACES, parts))

    across = [
        along_tensor(part[2, 1], 2, 0),
        along_tensor(part[1, 1], 1, 0),
        along_tensor(part[-1, 1], -1, 0),
    ]
    got = [
        along_tensor(part[2, 0], 2, 0),
        along_tensor(part[1, 0], 1, 0),
        along_tensor(part[-1, 0], -1, 0),
        along_tensor(added(part[0, 1], *across), 0, 1),
    ]

    keep, send = weight_partial(cot, blocks)
    both = exchanged(send, 1)
    total = added(keep[0], both[0], exchanged(added(keep[1], both[1]), 2))
    terms = [exchanged(total[2 * far : 2 * far + 2], 4 * far) for far in (1, 2, 3)]
    total = added(total[:2], *terms)
    total = added(total[0], exchanged(total[1], 16))
    home_pairs = [(there, here) for here, there in pairs]
    grad_weight = swapped(total, home_pairs).astype(F32).T

    home, guest = layer_out_of(migrate_plan, weight, blocks)
    returned = half_round(guest)
    layer_out = jnp.transpose(jnp.stack([home, returned]), (0, 2, 1))

    grads = (part[0, 0], *got)
    grad_qkv = backward(residue_counts, qkv, grads)
    return layer_out, jnp.transpose(grad_qkv, (0, 2, 1)), grad_weight


def solution(mesh):
    in_specs = (
        P(None, "dp", "tensor"),
        P("dp"),
        P("dp"),
        P("tensor", "dp"),
        P("dp", None, "tensor"),
    )
    out_specs = (P("dp", None, "tensor"), P(None, "dp", "tensor"), P("tensor", "dp"))
    return jax.shard_map(step, mesh=mesh, in_specs=in_specs, out_specs=out_specs, check_vma=False)
```
